32 devices in a mesh: freq: 4 (over y, x), param: 8 (over z, core).
Axes of the slice: x: 2, y: 2, z: 4, core: 2. Of those that a mesh axis runs over, the one named last changes fastest.
Arguments:
- chain_state: float32 [32, 2048, 512], P('freq', 'param'), may hold values from -6 to 6
- second_moment: float32 [32, 2048, 512], P('freq', 'param'), may hold values from 0.25 to 2
- noise: float32 [2, 32, 2048, 512], P(None, 'freq', 'param'), may hold values from -6 to 6
- green: bfloat16 [2, 64, 2048, 512], P(None, 'freq', 'param'), may hold values from -0.125 to 0.125
- observed: float32 [64, 1024], P('freq'), may hold values from -6 to 6
- inv_noise: float32 [64, 512], P('freq'), may hold values from 0.3 to 3
- temper: float32 [32], P('freq'), may hold values from 0.2 to 1
Outputs:
- new_state: float32 [32, 2048, 512], P('freq', 'param')
- new_moment: float32 [32, 2048, 512], P('freq', 'param')
The draws below stay inside these ranges and needn't reach their ends.
All inputs are finite; a program needn't handle non-finite values.
Results may differ from the reference program's by a relative error of at most 0.005.
Values may be sent and summed in bfloat16 or wider, within the bound.
A program may use at most 128 MiB of HBM per device.

```python
import math
import jax
import jax.numpy as jnp
from jax import lax

P_SIZE = 2048
NT = 512
F = 64
S = 512
C = 32
STEPS = 2


def with_spikes(result, key, source, target, blocks, factor):
    def block_of(dim):
        return (jnp.arange(result.shape[dim]) // (result.shape[dim] // blocks)).reshape((-1,) + (1,) * (result.ndim - 1 - dim))

    near = jax.random.permutation(key, blocks)[block_of(target)]
    other_side = (block_of(target) + blocks // 2) % blocks
    return jnp.where((block_of(source) == near) | (block_of(source) == other_side), factor * result, result)


def levels(stream_key, extent, split, smallest, largest):
    level, own = 1.0, jax.random.fold_in(stream_key, 6)
    for dim, parts in split:
        steps = jnp.exp(jax.random.uniform(jax.random.fold_in(own, dim), (parts,), jnp.float32, smallest / len(split), largest / len(split)))
        level = level * jnp.repeat(steps, extent[dim] // parts).reshape([-1 if axis == dim else 1 for axis in range(len(extent))])
    return level


def scatter_about(stream_key, dims, scale, limit, shards=(), kind=jnp.bfloat16):
    result = scale * jax.random.normal(stream_key, dims, jnp.float32)
    if shards:
        result = result * levels(stream_key, dims, shards, -0.22, 0.18)
    return jnp.clip(result, -limit, limit).astype(kind)


def heavy_noise(rng, shape, scale, most, shards, heavy, kind=jnp.bfloat16):
    entries = scale * jax.random.normal(rng, shape, jnp.float32)
    if shards:
        entries = entries * levels(rng, shape, shards, -0.22, 0.18)
    return jnp.clip(with_spikes(entries, jax.random.fold_in(rng, 3), *heavy), -most, most).astype(kind)


def setup_inputs(seed: int = 0) -> dict:
    seeds = jax.random.split(jax.random.key(seed), 8)
    return {
        "chain_state": scatter_about(seeds[0], (C, P_SIZE, NT), 1.0, 6.0, ((0, 4), (1, 8)), jnp.float32),
        "second_moment": jnp.clip(jnp.exp(math.log(2.0) - 2.0794415 * jax.random.uniform(seeds[1], (C, P_SIZE, NT), jnp.float32) ** levels(seeds[1], (C, P_SIZE, NT), ((0, 4), (1, 8)), -0.2, 0.2)), 0.25, 2.0),
        "noise": scatter_about(seeds[2], (STEPS, C, P_SIZE, NT), 1.0, 6.0, ((1, 4), (2, 8)), jnp.float32),
        "green": heavy_noise(seeds[3], (2, F, P_SIZE, S), (2 * P_SIZE) ** -0.5, 0.125, ((1, 4), (2, 8)), (2, 3, 8, 2.0)),
        "observed": scatter_about(seeds[4], (F, 2 * S), 1.0, 6.0, ((0, 4),), jnp.float32),
        "inv_noise": jnp.clip(jnp.exp(math.log(3.0) - 2.3025851 * jax.random.uniform(seeds[5], (F, S), jnp.float32) ** levels(seeds[5], (F, S), ((0, 4),), -0.2, 0.2)), 0.3, 3.0),
        "temper": jnp.clip(jnp.exp(math.log(1.0) - 1.609438 * jax.random.uniform(seeds[6], (C,), jnp.float32) ** levels(seeds[6], (C,), ((0, 4),), -0.2, 0.2)), 0.2, 1.0),
    }


decay_rate = 0.9
step_length = 0.5

def spectral_table(time_len, freq_total):
    time_index = jnp.arange(time_len, dtype=jnp.int32)[:, None]
    wave_number = jnp.arange(freq_total, dtype=jnp.int32)[None, :] + 1
    phase_angle = (time_index * wave_number % time_len).astype(jnp.float32) * (2.0 * math.pi / time_len)
    columns_table = jnp.stack([jnp.cos(phase_angle), -jnp.sin(phase_angle)], axis=-1).reshape(time_len, 2 * freq_total)
    return (columns_table / math.sqrt(time_len)).astype(jnp.bfloat16)

def per_frequency(inputs):
    real_in, imag_in, green_re, green_im, target, weight_row = inputs
    data_re = jnp.dot(real_in, green_re, preferred_element_type=jnp.float32) - jnp.dot(imag_in, green_im, preferred_element_type=jnp.float32)
    data_im = jnp.dot(real_in, green_im, preferred_element_type=jnp.float32) + jnp.dot(imag_in, green_re, preferred_element_type=jnp.float32)
    resid_re = (weight_row[:S] * (data_re - target[:S])).astype(jnp.bfloat16)
    resid_im = (weight_row[S:] * (data_im - target[S:])).astype(jnp.bfloat16)
    back_re = jnp.dot(resid_re, green_re.T, preferred_element_type=jnp.float32) + jnp.dot(resid_im, green_im.T, preferred_element_type=jnp.float32)
    back_im = jnp.dot(resid_im, green_re.T, preferred_element_type=jnp.float32) - jnp.dot(resid_re, green_im.T, preferred_element_type=jnp.float32)
    return (back_re.astype(jnp.bfloat16), back_im.astype(jnp.bfloat16))

def reference(chain_state, second_moment, noise, green, observed, inv_noise, temper):
    forward_table = spectral_table(NT, F)
    current = chain_state
    moment = second_moment
    weights_full = jnp.concatenate([inv_noise, inv_noise], axis=1)
    for step_num in range(STEPS):
        low_state = current.astype(jnp.bfloat16)
        spectrum = jnp.dot(low_state.reshape(C * P_SIZE, NT), forward_table, preferred_element_type=jnp.float32)
        spectrum = spectrum.astype(jnp.bfloat16).reshape(C, P_SIZE, F, 2)
        real_part = spectrum[..., 0].transpose(2, 0, 1)
        imag_part = spectrum[..., 1].transpose(2, 0, 1)
        back_re, back_im = lax.map(per_frequency, (real_part, imag_part, green[0], green[1], observed, weights_full))
        adjoint = jnp.stack([back_re, back_im], axis=-1).transpose(1, 2, 0, 3).reshape(C * P_SIZE, 2 * F)
        gradient = jnp.dot(adjoint, forward_table.T, preferred_element_type=jnp.float32).reshape(C, P_SIZE, NT)
        drift_term = temper[:, None, None] * gradient + current
        moment = decay_rate * moment + (1.0 - decay_rate) * drift_term * drift_term
        precondition = lax.rsqrt(moment)
        current = current - step_length * precondition * drift_term + math.sqrt(2.0 * step_length) * jnp.sqrt(precondition) * noise[step_num]
    return (current, moment)
```

```python
import functools
import math

import jax
import jax.numpy as jnp
from jax import lax
from jax.experimental import pallas as pl
from jax.experimental.pallas import tpu as pltpu
from jax.sharding import PartitionSpec as P

decay_rate = 0.9
step_length = 0.5
MESH = pl.DeviceIdType.MESH
LANES = 128
CHUNK_FREQS = 2


def spectral_table(time_len, freq_total):
    time_index = jnp.arange(time_len, dtype=jnp.int32)[:, None]
    wave_number = jnp.arange(freq_total, dtype=jnp.int32)[None, :] + 1
    phase_angle = (time_index * wave_number % time_len).astype(jnp.float32) * (
        2.0 * math.pi / time_len
    )
    columns_table = jnp.stack([jnp.cos(phase_angle), -jnp.sin(phase_angle)], axis=-1).reshape(
        time_len, 2 * freq_total
    )
    return (columns_table / math.sqrt(time_len)).astype(jnp.bfloat16)


def exchange_kernel(
    freq_count, levels, chunk_freqs,
    spec_ref, green_hbm, obs_ref, inv_ref, own_ref,
    green, field, acc, outgoing, incoming, wtd, adj,
    green_sem, spec_send, spec_recv, red_send, red_recv, gat_send, gat_recv,
    adj_send, adj_recv, local_sem,
):
    freq_me = lax.axis_index("freq")
    param_me = lax.axis_index("param")
    freq_loc, rows = spec_ref.shape[1], spec_ref.shape[2]
    half_rows = rows // 2
    sensors = green.shape[3]
    col_blocks = sensors // LANES
    chunk_blocks = chunk_freqs * col_blocks
    chunks = freq_loc // chunk_freqs
    bits = [lax.rem(param_me // 2**k, 2) for k in range(levels)]
    partners = [param_me + (1 - 2 * bits[k]) * 2**k for k in range(levels)]
    lens = [chunk_blocks // 2**k for k in range(levels + 1)]
    offs = [0]
    for k in range(levels):
        offs.append(offs[k] + bits[k] * lens[k + 1])

    def freq_peer(d):
        return lax.rem(freq_me + d, freq_count)

    def freq_source(d):
        return lax.rem(freq_me + freq_count - d, freq_count)

    barrier = pltpu.get_barrier_semaphore()
    for d in range(1, freq_count):
        pl.semaphore_signal(barrier, inc=1, device_id={"freq": freq_peer(d)}, device_id_type=MESH)
    for k in range(levels):
        pl.semaphore_signal(barrier, inc=1, device_id={"param": partners[k]}, device_id_type=MESH)

    def green_copy(i):
        part = pl.ds(i * chunk_freqs, chunk_freqs)
        return pltpu.make_async_copy(green_hbm.at[:, part], green.at[:, part], green_sem.at[i])

    def own_spec_copy():
        return pltpu.make_async_copy(spec_ref.at[freq_me], field.at[:, freq_me], local_sem.at[0])

    def spec_copy(i, d):
        part = pl.ds(i * chunk_freqs, chunk_freqs)
        return pltpu.make_async_remote_copy(
            src_ref=spec_ref.at[freq_peer(d), part],
            dst_ref=field.at[part, freq_me],
            send_sem=spec_send.at[d - 1, i],
            recv_sem=spec_recv.at[d - 1, i],
            device_id={"freq": freq_peer(d)},
            device_id_type=MESH,
        )

    def reduce_copy(i, k):
        part = pl.ds(i * lens[k + 1], lens[k + 1])
        if k == 0:
            away = (1 - bits[0]) * lens[1]
            src = outgoing[0].at[pl.ds(i * chunk_blocks + away, lens[1])]
        else:
            src = outgoing[k].at[part]
        return pltpu.make_async_remote_copy(
            src_ref=src,
            dst_ref=incoming[k].at[part],
            send_sem=red_send.at[k, i],
            recv_sem=red_recv.at[k, i],
            device_id={"param": partners[k]},
            device_id_type=MESH,
        )

    def gather_copy(i, k):
        part = pl.ds(i * chunk_blocks + offs[k + 1], lens[k + 1])
        return pltpu.make_async_remote_copy(
            src_ref=wtd.at[part],
            dst_ref=wtd.at[part],
            send_sem=gat_send.at[k, i],
            recv_sem=gat_recv.at[k, i],
            device_id={"param": partners[k]},
            device_id_type=MESH,
        )

    def adj_copy(i, d):
        part = pl.ds(i * chunk_freqs, chunk_freqs)
        return pltpu.make_async_remote_copy(
            src_ref=adj.at[part, freq_peer(d)],
            dst_ref=own_ref.at[freq_me, part],
            send_sem=adj_send.at[d - 1, i],
            recv_sem=adj_recv.at[d - 1, i],
            device_id={"freq": freq_peer(d)},
            device_id_type=MESH,
        )

    def own_adj_copy(i):
        part = pl.ds(i * chunk_freqs, chunk_freqs)
        return pltpu.make_async_copy(
            adj.at[part, freq_me], own_ref.at[freq_me, part], local_sem.at[i + 1]
        )

    own_spec_copy().start()

    @pl.loop(0, chunks)
    def _(i):
        green_copy(i).start()

    pl.semaphore_wait(barrier, freq_count - 1 + levels)

    @pl.loop(0, chunks)
    def _(i):
        for d in range(1, freq_count):
            spec_copy(i, d).start()

    own_spec_copy().wait()

    def combine(first, second, sign):
        pieces = []
        for j in range(freq_count):
            for ri in range(2):
                here = j * rows + ri * half_rows
                there = j * rows + (1 - ri) * half_rows
                a = first[here : here + half_rows]
                b = second[there : there + half_rows]
                pieces.append(a + b if (ri == 1) == (sign > 0) else a - b)
        return jnp.concatenate(pieces, axis=0)

    def forward(i):
        green_copy(i).wait()
        for d in range(1, freq_count):
            spec_copy(i, d).wait_recv()
        for g in range(chunk_freqs):
            f = i * chunk_freqs + g
            x = field[f].reshape(freq_count * rows, field.shape[3])
            first = jnp.dot(x, green[0, f], preferred_element_type=jnp.float32)
            second = jnp.dot(x, green[1, f], preferred_element_type=jnp.float32)
            data = combine(first, second, 1)
            for b in range(col_blocks):
                block = data[:, b * LANES : (b + 1) * LANES]
                acc[f * col_blocks + b] = block
                outgoing[0][f * col_blocks + b] = block.astype(jnp.bfloat16)
        reduce_copy(i, 0).start()

    def reduce(i, k):
        reduce_copy(i, k - 1).wait_recv()
        kept = pl.ds(i * chunk_blocks + offs[k], lens[k])
        acc[kept] = acc[kept] + incoming[k - 1][pl.ds(i * lens[k], lens[k])].astype(jnp.float32)
        away = offs[k] + (1 - bits[k]) * lens[k + 1]
        outgoing[k][pl.ds(i * lens[k + 1], lens[k + 1])] = acc[
            pl.ds(i * chunk_blocks + away, lens[k + 1])
        ].astype(jnp.bfloat16)
        reduce_copy(i, k).start()

    def weigh(i):
        reduce_copy(i, levels - 1).wait_recv()
        for n in range(lens[levels]):
            b = i * chunk_blocks + offs[levels] + n
            total = acc[b] + incoming[levels - 1][i * lens[levels] + n].astype(jnp.float32)
            target = obs_ref[b]
            weight = inv_ref[b]
            pieces = []
            for j in range(freq_count):
                for ri in range(2):
                    here = j * rows + ri * half_rows
                    pieces.append(
                        weight * (total[here : here + half_rows] - target[ri : ri + 1])
                    )
            wtd[b] = jnp.concatenate(pieces, axis=0).astype(jnp.bfloat16)
        gather_copy(i, levels - 1).start()

    def gather(i, k):
        gather_copy(i, k).wait_recv()
        gather_copy(i, k - 1).start()

    def backward(i):
        gather_copy(i, 0).wait_recv()
        dims = (((1,), (1,)), ((), ()))
        for g in range(chunk_freqs):
            f = i * chunk_freqs + g
            w = jnp.concatenate([wtd[f * col_blocks + b] for b in range(col_blocks)], axis=1)
            first = lax.dot_general(w, green[0, f], dims, preferred_element_type=jnp.float32)
            second = lax.dot_general(w, green[1, f], dims, preferred_element_type=jnp.float32)
            back = combine(first, second, -1).astype(jnp.bfloat16)
            adj[f] = back.reshape(freq_count, rows, back.shape[1])
        for d in range(1, freq_count):
            adj_copy(i, d).start()
        own_adj_copy(i).start()

    stages = [forward]
    for k in range(1, levels):
        stages.append(functools.partial(reduce, k=k))
    stages.append(weigh)
    for k in range(levels - 1, 0, -1):
        stages.append(functools.partial(gather, k=k))
    stages.append(backward)

    @pl.loop(0, chunks + len(stages) - 1)
    def _(tick):
        for lag, stage in enumerate(stages):
            @pl.when((tick >= lag) & (tick < chunks + lag))
            def _():
                stage(tick - lag)

    @pl.loop(0, chunks)
    def _(i):
        for d in range(1, freq_count):
            spec_copy(i, d).wait_send()
        for k in range(levels):
            reduce_copy(i, k).wait_send()
            gather_copy(i, k).wait_send()
        for d in range(1, freq_count):
            adj_copy(i, d).wait_send()
            adj_copy(i, d).wait_recv()
        own_adj_copy(i).wait()


def exchange(spec, green, obs_blocks, inv_blocks, call_id):
    freq_count, freq_loc, rows, slab = spec.shape
    levels = int(math.log2(lax.axis_size("param")))
    sensors = green.shape[3]
    col_blocks = sensors // LANES
    chunk_blocks = CHUNK_FREQS * col_blocks
    chunks = freq_loc // CHUNK_FREQS
    blocks = freq_loc * col_blocks
    all_rows = freq_count * rows
    bf16, f32 = jnp.bfloat16, jnp.float32
    piece = [blocks // 2 ** (k + 1) for k in range(levels)]
    dma = pltpu.SemaphoreType.DMA
    vmem = pl.BlockSpec(memory_space=pltpu.VMEM)
    flops = 16 * freq_loc * all_rows * slab * sensors
    return pl.pallas_call(
        functools.partial(exchange_kernel, freq_count, levels, CHUNK_FREQS),
        out_shape=jax.ShapeDtypeStruct(spec.shape, bf16),
        in_specs=[vmem, pl.BlockSpec(memory_space=pl.ANY), vmem, vmem],
        out_specs=vmem,
        scratch_shapes=[
            pltpu.VMEM(green.shape, bf16),
            pltpu.VMEM((freq_loc, freq_count, rows, slab), bf16),
            pltpu.VMEM((blocks, all_rows, LANES), f32),
            [
                pltpu.VMEM((blocks if k == 0 else piece[k], all_rows, LANES), bf16)
                for k in range(levels)
            ],
            [pltpu.VMEM((piece[k], all_rows, LANES), bf16) for k in range(levels)],
            pltpu.VMEM((blocks, all_rows, LANES), bf16),
            pltpu.VMEM((freq_loc, freq_count, rows, slab), bf16),
            dma((chunks,)),
            dma((freq_count - 1, chunks)),
            dma((freq_count - 1, chunks)),
            dma((levels, chunks)),
            dma((levels, chunks)),
            dma((levels, chunks)),
            dma((levels, chunks)),
            dma((freq_count - 1, chunks)),
            dma((freq_count - 1, chunks)),
            dma((chunks + 1,)),
        ],
        compiler_params=pltpu.CompilerParams(
            collective_id=call_id, has_side_effects=True, vmem_limit_bytes=40 * 2**20
        ),
        cost_estimate=pl.CostEstimate(
            flops=flops, bytes_accessed=2 * green.size, transcendentals=0
        ),
    )(spec, green, obs_blocks, inv_blocks)


def fits_kernel(chain_shape, green_shape):
    chains_loc, slab = chain_shape[0], chain_shape[1]
    param_count = lax.axis_size("param")
    blocks = CHUNK_FREQS * (green_shape[3] // LANES)
    return (
        2 * chains_loc % 16 == 0
        and slab % LANES == 0
        and green_shape[3] % LANES == 0
        and green_shape[1] % CHUNK_FREQS == 0
        and param_count & (param_count - 1) == 0
        and param_count > 1
        and lax.axis_size("freq") > 1
        and blocks % param_count == 0
    )


def kernel_steps(chain_state, second_moment, noise, green, observed, inv_noise, temper):
    chains_loc, slab_rows, time_len = chain_state.shape
    freq_loc, sensors = green.shape[1], green.shape[3]
    freq_count = lax.axis_size("freq")
    freq_total = freq_loc * freq_count
    table = spectral_table(time_len, freq_total)
    col_blocks = sensors // LANES
    obs_blocks = (
        observed.reshape(freq_loc, 2, col_blocks, LANES)
        .transpose(0, 2, 1, 3)
        .reshape(freq_loc * col_blocks, 2, LANES)
    )
    inv_blocks = inv_noise.reshape(freq_loc * col_blocks, 1, LANES)
    temper_cols = temper[:, None, None]
    current = chain_state
    moment = second_moment
    for step_num in range(noise.shape[0]):
        spec = jnp.einsum(
            "cpt,tj->jcp",
            current.astype(jnp.bfloat16),
            table,
            preferred_element_type=jnp.float32,
        ).astype(jnp.bfloat16)
        spec = spec.reshape(freq_count, freq_loc, 2 * chains_loc, slab_rows)
        own_adjoint = exchange(spec, green, obs_blocks, inv_blocks, step_num)
        gradient = jnp.einsum(
            "jcp,tj->cpt",
            own_adjoint.reshape(2 * freq_total, chains_loc, slab_rows),
            table,
            preferred_element_type=jnp.float32,
        )
        drift_term = temper_cols * gradient + current
        moment = decay_rate * moment + (1.0 - decay_rate) * drift_term * drift_term
        precondition = lax.rsqrt(moment)
        current = (
            current
            - step_length * precondition * drift_term
            + math.sqrt(2.0 * step_length) * jnp.sqrt(precondition) * noise[step_num]
        )
    return (current, moment)


def on_device(chain_state, second_moment, noise, green, observed, inv_noise, temper):
    if fits_kernel(chain_state.shape, green.shape):
        return kernel_steps(
            chain_state, second_moment, noise, green, observed, inv_noise, temper
        )
    chains_loc, slab_rows, time_len = chain_state.shape
    freq_loc = green.shape[1]
    freq_count = lax.axis_size("freq")
    freq_total = freq_loc * freq_count
    chains = chains_loc * freq_count
    forward_table = spectral_table(time_len, freq_total)
    inverse_table = forward_table.T
    green_re = green[0]
    green_im = green[1]
    upper_rows = jnp.concatenate([green_re, green_im], axis=2)
    lower_rows = jnp.concatenate([-green_im, green_re], axis=2)
    kernel = jnp.concatenate([upper_rows, lower_rows], axis=1)
    weights = jnp.concatenate([inv_noise, inv_noise], axis=1)
    temper_cols = temper[:, None, None]
    current = chain_state
    moment = second_moment
    for step_num in range(noise.shape[0]):
        low_state = current.astype(jnp.bfloat16)
        local_spec = jnp.dot(
            low_state.reshape(chains_loc * slab_rows, time_len),
            forward_table,
            preferred_element_type=jnp.float32,
        )
        local_spec = local_spec.astype(jnp.bfloat16).reshape(chains_loc, slab_rows, 2 * freq_total)
        spectrum = lax.all_to_all(local_spec, "freq", split_axis=2, concat_axis=0, tiled=True)
        mixed_spec = (
            spectrum.reshape(chains, slab_rows, freq_loc, 2)
            .transpose(2, 0, 3, 1)
            .reshape(freq_loc, chains, 2 * slab_rows)
        )
        partial_data = jnp.einsum(
            "fcq,fqs->fcs", mixed_spec, kernel, preferred_element_type=jnp.float32
        )
        predicted = lax.psum(partial_data.astype(jnp.bfloat16), "param").astype(jnp.float32)
        weighted = (weights[:, None, :] * (predicted - observed[:, None, :])).astype(jnp.bfloat16)
        adjoint = jnp.einsum(
            "fcs,fqs->fcq", weighted, kernel, preferred_element_type=jnp.float32
        ).astype(jnp.bfloat16)
        adjoint = (
            adjoint.reshape(freq_loc, chains, 2, slab_rows)
            .transpose(1, 3, 0, 2)
            .reshape(chains, slab_rows, 2 * freq_loc)
        )
        own_adjoint = lax.all_to_all(adjoint, "freq", split_axis=0, concat_axis=2, tiled=True)
        gradient = jnp.dot(
            own_adjoint.reshape(chains_loc * slab_rows, 2 * freq_total),
            inverse_table,
            preferred_element_type=jnp.float32,
        )
        gradient = gradient.reshape(chains_loc, slab_rows, time_len)
        drift_term = temper_cols * gradient + current
        moment = decay_rate * moment + (1.0 - decay_rate) * drift_term * drift_term
        precondition = lax.rsqrt(moment)
        current = (
            current
            - step_length * precondition * drift_term
            + math.sqrt(2.0 * step_length) * jnp.sqrt(precondition) * noise[step_num]
        )
    return (current, moment)


def solution(mesh):
    return jax.shard_map(
        on_device,
        mesh=mesh,
        in_specs=(
            P("freq", "param", None),
            P("freq", "param", None),
            P(None, "freq", "param", None),
            P(None, "freq", "param", None),
            P("freq", None),
            P("freq", None),
            P("freq"),
        ),
        out_specs=(P("freq", "param", None), P("freq", "param", None)),
        check_vma=False,
    )
```

```python
import functools
import math

import jax
import jax.numpy as jnp
from jax import lax
from jax.experimental import pallas as pl
from jax.experimental.pallas import tpu as pltpu
from jax.sharding import PartitionSpec as P

decay_rate = 0.9
step_length = 0.5
MESH = pl.DeviceIdType.MESH
LANES = 128
CHUNK_FREQS = 2
STAGE_TICKS = (0, 1, 3, 5, 7, 9, 10)


def spectral_table(time_len, freq_total):
    time_index = jnp.arange(time_len, dtype=jnp.int32)[:, None]
    wave_number = jnp.arange(freq_total, dtype=jnp.int32)[None, :] + 1
    phase_angle = (time_index * wave_number % time_len).astype(jnp.float32) * (
        2.0 * math.pi / time_len
    )
    columns_table = jnp.stack([jnp.cos(phase_angle), -jnp.sin(phase_angle)], axis=-1).reshape(
        time_len, 2 * freq_total
    )
    return (columns_table / math.sqrt(time_len)).astype(jnp.bfloat16)


def exchange_kernel(
    freq_count, chunk_freqs, stage_ticks,
    spec_ref, green_hbm, obs_ref, inv_ref, own_ref,
    green, field, acc, outgoing, incoming, wtd, adj,
    green_sem, spec_send, spec_recv, line_send, line_recv, adj_send, adj_recv, local_sem,
):
    freq_me = lax.axis_index("freq")
    param_me = lax.axis_index("param")
    freq_loc, rows = spec_ref.shape[1], spec_ref.shape[2]
    half_rows = rows // 2
    sensors = green.shape[3]
    col_blocks = sensors // LANES
    chunk_blocks = chunk_freqs * col_blocks
    chunks = freq_loc // chunk_freqs
    core = lax.rem(param_me, 2)
    chip = param_me // 2
    side = chip // 2
    outer = (chip + side) % 2 == 0
    inner = (chip + side) % 2 == 1
    core_peer = param_me + 1 - 2 * core
    chip_peer = param_me + 2 * (1 - 2 * lax.rem(chip, 2))
    mid_peer = param_me + 2 * (1 - 2 * side)
    core_len, mid_len = chunk_blocks // 2, chunk_blocks // 4
    core_off = core * core_len
    mid_off = core_off + side * mid_len

    def freq_peer(d):
        return lax.rem(freq_me + d, freq_count)

    def freq_source(d):
        return lax.rem(freq_me + freq_count - d, freq_count)

    barrier = pltpu.get_barrier_semaphore()
    for d in range(1, freq_count):
        pl.semaphore_signal(barrier, inc=1, device_id={"freq": freq_peer(d)}, device_id_type=MESH)
    for peer in (core_peer, chip_peer):
        pl.semaphore_signal(barrier, inc=1, device_id={"param": peer}, device_id_type=MESH)

    @pl.when(inner)
    def _():
        pl.semaphore_signal(barrier, inc=1, device_id={"param": mid_peer}, device_id_type=MESH)

    def green_copy(i):
        part = pl.ds(i * chunk_freqs, chunk_freqs)
        return pltpu.make_async_copy(green_hbm.at[:, part], green.at[:, part], green_sem.at[i])

    def own_spec_copy():
        return pltpu.make_async_copy(spec_ref.at[freq_me], field.at[:, freq_me], local_sem.at[0])

    def spec_copy(i, d):
        part = pl.ds(i * chunk_freqs, chunk_freqs)
        return pltpu.make_async_remote_copy(
            src_ref=spec_ref.at[freq_peer(d), part],
            dst_ref=field.at[part, freq_me],
            send_sem=spec_send.at[d - 1, i],
            recv_sem=spec_recv.at[d - 1, i],
            device_id={"freq": freq_peer(d)},
            device_id_type=MESH,
        )

    def param_copy(k, i, src, dst, peer):
        return pltpu.make_async_remote_copy(
            src_ref=src,
            dst_ref=dst,
            send_sem=line_send.at[k, i],
            recv_sem=line_recv.at[k, i],
            device_id={"param": peer},
            device_id_type=MESH,
        )

    def core_reduce(i):
        src = outgoing[0].at[pl.ds(i * chunk_blocks + (1 - core) * core_len, core_len)]
        return param_copy(0, i, src, incoming[0].at[pl.ds(i * core_len, core_len)], core_peer)

    def chip_reduce(i):
        part = pl.ds(i * core_len, core_len)
        return param_copy(1, i, outgoing[1].at[part], incoming[1].at[part], chip_peer)

    def mid_reduce(i):
        part = pl.ds(i * mid_len, mid_len)
        return param_copy(2, i, outgoing[2].at[part], incoming[2].at[part], mid_peer)

    def mid_gather(i):
        part = wtd.at[pl.ds(i * chunk_blocks + mid_off, mid_len)]
        return param_copy(3, i, part, part, mid_peer)

    def chip_gather(i):
        part = wtd.at[pl.ds(i * chunk_blocks + core_off, core_len)]
        return param_copy(4, i, part, part, chip_peer)

    def core_gather(i):
        part = wtd.at[pl.ds(i * chunk_blocks + core_off, core_len)]
        return param_copy(5, i, part, part, core_peer)

    def adj_copy(i, d):
        part = pl.ds(i * chunk_freqs, chunk_freqs)
        return pltpu.make_async_remote_copy(
            src_ref=adj.at[part, freq_peer(d)],
            dst_ref=own_ref.at[freq_me, part],
            send_sem=adj_send.at[d - 1, i],
            recv_sem=adj_recv.at[d - 1, i],
            device_id={"freq": freq_peer(d)},
            device_id_type=MESH,
        )

    def own_adj_copy(i):
        part = pl.ds(i * chunk_freqs, chunk_freqs)
        return pltpu.make_async_copy(
            adj.at[part, freq_me], own_ref.at[freq_me, part], local_sem.at[i + 1]
        )

    own_spec_copy().start()

    @pl.loop(0, chunks)
    def _(i):
        green_copy(i).start()

    pl.semaphore_wait(barrier, freq_count + 1 + (chip + side) % 2)

    @pl.loop(0, chunks)
    def _(i):
        for d in range(1, freq_count):
            spec_copy(i, d).start()

    own_spec_copy().wait()

    def combine(first, second, sign):
        pieces = []
        for j in range(freq_count):
            for ri in range(2):
                here = j * rows + ri * half_rows
                there = j * rows + (1 - ri) * half_rows
                a = first[here : here + half_rows]
                b = second[there : there + half_rows]
                pieces.append(a + b if (ri == 1) == (sign > 0) else a - b)
        return jnp.concatenate(pieces, axis=0)

    def forward(i):
        green_copy(i).wait()
        for d in range(1, freq_count):
            spec_copy(i, d).wait_recv()
        for g in range(chunk_freqs):
            f = i * chunk_freqs + g
            x = field[f].reshape(freq_count * rows, field.shape[3])
            first = jnp.dot(x, green[0, f], preferred_element_type=jnp.float32)
            second = jnp.dot(x, green[1, f], preferred_element_type=jnp.float32)
            data = combine(first, second, 1)
            for b in range(col_blocks):
                block = data[:, b * LANES : (b + 1) * LANES]
                acc[f * col_blocks + b] = block
                outgoing[0][f * col_blocks + b] = block.astype(jnp.bfloat16)
        core_reduce(i).start()

    def pass_inward(i):
        core_reduce(i).wait_recv()
        kept = pl.ds(i * chunk_blocks + core_off, core_len)
        part = pl.ds(i * core_len, core_len)
        total = acc[kept] + incoming[0][part].astype(jnp.float32)

        @pl.when(inner)
        def _():
            acc[kept] = total

        @pl.when(outer)
        def _():
            outgoing[1][part] = total.astype(jnp.bfloat16)
            chip_reduce(i).start()

    def cross(i):
        @pl.when(inner)
        def _():
            chip_reduce(i).wait_recv()
            kept = pl.ds(i * chunk_blocks + core_off, core_len)
            part = pl.ds(i * core_len, core_len)
            acc[kept] = acc[kept] + incoming[1][part].astype(jnp.float32)
            away = pl.ds(i * chunk_blocks + core_off + (1 - side) * mid_len, mid_len)
            outgoing[2][pl.ds(i * mid_len, mid_len)] = acc[away].astype(jnp.bfloat16)
            mid_reduce(i).start()

    def weigh(i):
        @pl.when(inner)
        def _():
            mid_reduce(i).wait_recv()
            for n in range(mid_len):
                b = i * chunk_blocks + mid_off + n
                total = acc[b] + incoming[2][i * mid_len + n].astype(jnp.float32)
                target = obs_ref[b]
                weight = inv_ref[b]
                pieces = []
                for j in range(freq_count):
                    for ri in range(2):
                        here = j * rows + ri * half_rows
                        pieces.append(
                            weight * (total[here : here + half_rows] - target[ri : ri + 1])
                        )
                wtd[b] = jnp.concatenate(pieces, axis=0).astype(jnp.bfloat16)
            mid_gather(i).start()

    def pass_outward(i):
        @pl.when(inner)
        def _():
            mid_gather(i).wait_recv()
            chip_gather(i).start()
            core_gather(i).start()

    def share(i):
        @pl.when(outer)
        def _():
            chip_gather(i).wait_recv()
            core_gather(i).start()

    def backward(i):
        core_gather(i).wait_recv()
        dims = (((1,), (1,)), ((), ()))
        for g in range(chunk_freqs):
            f = i * chunk_freqs + g
            w = jnp.concatenate([wtd[f * col_blocks + b] for b in range(col_blocks)], axis=1)
            first = lax.dot_general(w, green[0, f], dims, preferred_element_type=jnp.float32)
            second = lax.dot_general(w, green[1, f], dims, preferred_element_type=jnp.float32)
            back = combine(first, second, -1).astype(jnp.bfloat16)
            adj[f] = back.reshape(freq_count, rows, back.shape[1])
        for d in range(1, freq_count):
            adj_copy(i, d).start()
        own_adj_copy(i).start()

    stages = (forward, pass_inward, cross, weigh, pass_outward, share, backward)

    @pl.loop(0, chunks + stage_ticks[-1])
    def _(tick):
        for lag, stage in zip(stage_ticks, stages):
            @pl.when((tick >= lag) & (tick < chunks + lag))
            def _():
                stage(tick - lag)

    @pl.loop(0, chunks)
    def _(i):
        for d in range(1, freq_count):
            spec_copy(i, d).wait_send()
        core_reduce(i).wait_send()
        core_gather(i).wait_send()

        @pl.when(outer)
        def _():
            chip_reduce(i).wait_send()

        @pl.when(inner)
        def _():
            mid_reduce(i).wait_send()
            mid_gather(i).wait_send()
            chip_gather(i).wait_send()

        for d in range(1, freq_count):
            adj_copy(i, d).wait_send()
            adj_copy(i, d).wait_recv()
        own_adj_copy(i).wait()


def exchange(spec, green, obs_blocks, inv_blocks, call_id):
    freq_count, freq_loc, rows, slab = spec.shape
    sensors = green.shape[3]
    col_blocks = sensors // LANES
    chunk_blocks = CHUNK_FREQS * col_blocks
    chunks = freq_loc // CHUNK_FREQS
    blocks = freq_loc * col_blocks
    all_rows = freq_count * rows
    bf16, f32 = jnp.bfloat16, jnp.float32
    dma = pltpu.SemaphoreType.DMA
    vmem = pl.BlockSpec(memory_space=pltpu.VMEM)
    flops = 16 * freq_loc * all_rows * slab * sensors
    return pl.pallas_call(
        functools.partial(exchange_kernel, freq_count, CHUNK_FREQS, STAGE_TICKS),
        out_shape=jax.ShapeDtypeStruct(spec.shape, bf16),
        in_specs=[vmem, pl.BlockSpec(memory_space=pltpu.HBM), vmem, vmem],
        out_specs=vmem,
        scratch_shapes=[
            pltpu.VMEM(green.shape, bf16),
            pltpu.VMEM((freq_loc, freq_count, rows, slab), bf16),
            pltpu.VMEM((blocks, all_rows, LANES), f32),
            [pltpu.VMEM((blocks // part, all_rows, LANES), bf16) for part in (1, 2, 4)],
            [pltpu.VMEM((blocks // part, all_rows, LANES), bf16) for part in (2, 2, 4)],
            pltpu.VMEM((blocks, all_rows, LANES), bf16),
            pltpu.VMEM((freq_loc, freq_count, rows, slab), bf16),
            dma((chunks,)),
            dma((freq_count - 1, chunks)),
            dma((freq_count - 1, chunks)),
            dma((6, chunks)),
            dma((6, chunks)),
            dma((freq_count - 1, chunks)),
            dma((freq_count - 1, chunks)),
            dma((chunks + 1,)),
        ],
        compiler_params=pltpu.CompilerParams(
            collective_id=call_id, has_side_effects=True, vmem_limit_bytes=40 * 2**20
        ),
        cost_estimate=pl.CostEstimate(
            flops=flops, bytes_accessed=2 * green.size, transcendentals=0
        ),
    )(spec, green, obs_blocks, inv_blocks)


def fits_kernel(chain_shape, green_shape):
    chains_loc, slab = chain_shape[0], chain_shape[1]
    param_count = lax.axis_size("param")
    blocks = CHUNK_FREQS * (green_shape[3] // LANES)
    return (
        2 * chains_loc % 16 == 0
        and slab % LANES == 0
        and green_shape[3] % LANES == 0
        and green_shape[1] % CHUNK_FREQS == 0
        and param_count == 8
        and lax.axis_size("freq") > 1
        and blocks % 4 == 0
    )


def kernel_steps(chain_state, second_moment, noise, green, observed, inv_noise, temper):
    chains_loc, slab_rows, time_len = chain_state.shape
    freq_loc, sensors = green.shape[1], green.shape[3]
    freq_count = lax.axis_size("freq")
    freq_total = freq_loc * freq_count
    table = spectral_table(time_len, freq_total)
    col_blocks = sensors // LANES
    obs_blocks = (
        observed.reshape(freq_loc, 2, col_blocks, LANES)
        .transpose(0, 2, 1, 3)
        .reshape(freq_loc * col_blocks, 2, LANES)
    )
    inv_blocks = inv_noise.reshape(freq_loc * col_blocks, 1, LANES)
    temper_cols = temper[:, None, None]
    current = chain_state
    moment = second_moment
    for step_num in range(noise.shape[0]):
        spec = jnp.einsum(
            "cpt,tj->jcp",
            current.astype(jnp.bfloat16),
            table,
            preferred_element_type=jnp.float32,
        ).astype(jnp.bfloat16)
        spec = spec.reshape(freq_count, freq_loc, 2 * chains_loc, slab_rows)
        own_adjoint = exchange(spec, green, obs_blocks, inv_blocks, step_num)
        gradient = jnp.einsum(
            "jcp,tj->cpt",
            own_adjoint.reshape(2 * freq_total, chains_loc, slab_rows),
            table,
            preferred_element_type=jnp.float32,
        )
        drift_term = temper_cols * gradient + current
        moment = decay_rate * moment + (1.0 - decay_rate) * drift_term * drift_term
        precondition = lax.rsqrt(moment)
        current = (
            current
            - step_length * precondition * drift_term
            + math.sqrt(2.0 * step_length) * jnp.sqrt(precondition) * noise[step_num]
        )
    return (current, moment)


def on_device(chain_state, second_moment, noise, green, observed, inv_noise, temper):
    if fits_kernel(chain_state.shape, green.shape):
        return kernel_steps(
            chain_state, second_moment, noise, green, observed, inv_noise, temper
        )
    chains_loc, slab_rows, time_len = chain_state.shape
    freq_loc = green.shape[1]
    freq_count = lax.axis_size("freq")
    freq_total = freq_loc * freq_count
    chains = chains_loc * freq_count
    forward_table = spectral_table(time_len, freq_total)
    inverse_table = forward_table.T
    green_re = green[0]
    green_im = green[1]
    upper_rows = jnp.concatenate([green_re, green_im], axis=2)
    lower_rows = jnp.concatenate([-green_im, green_re], axis=2)
    kernel = jnp.concatenate([upper_rows, lower_rows], axis=1)
    weights = jnp.concatenate([inv_noise, inv_noise], axis=1)
    temper_cols = temper[:, None, None]
    current = chain_state
    moment = second_moment
    for step_num in range(noise.shape[0]):
        low_state = current.astype(jnp.bfloat16)
        local_spec = jnp.dot(
            low_state.reshape(chains_loc * slab_rows, time_len),
            forward_table,
            preferred_element_type=jnp.float32,
        )
        local_spec = local_spec.astype(jnp.bfloat16).reshape(chains_loc, slab_rows, 2 * freq_total)
        spectrum = lax.all_to_all(local_spec, "freq", split_axis=2, concat_axis=0, tiled=True)
        mixed_spec = (
            spectrum.reshape(chains, slab_rows, freq_loc, 2)
            .transpose(2, 0, 3, 1)
            .reshape(freq_loc, chains, 2 * slab_rows)
        )
        partial_data = jnp.einsum(
            "fcq,fqs->fcs", mixed_spec, kernel, preferred_element_type=jnp.float32
        )
        predicted = lax.psum(partial_data.astype(jnp.bfloat16), "param").astype(jnp.float32)
        weighted = (weights[:, None, :] * (predicted - observed[:, None, :])).astype(jnp.bfloat16)
        adjoint = jnp.einsum(
            "fcs,fqs->fcq", weighted, kernel, preferred_element_type=jnp.float32
        ).astype(jnp.bfloat16)
        adjoint = (
            adjoint.reshape(freq_loc, chains, 2, slab_rows)
            .transpose(1, 3, 0, 2)
            .reshape(chains, slab_rows, 2 * freq_loc)
        )
        own_adjoint = lax.all_to_all(adjoint, "freq", split_axis=0, concat_axis=2, tiled=True)
        gradient = jnp.dot(
            own_adjoint.reshape(chains_loc * slab_rows, 2 * freq_total),
            inverse_table,
            preferred_element_type=jnp.float32,
        )
        gradient = gradient.reshape(chains_loc, slab_rows, time_len)
        drift_term = temper_cols * gradient + current
        moment = decay_rate * moment + (1.0 - decay_rate) * drift_term * drift_term
        precondition = lax.rsqrt(moment)
        current = (
            current
            - step_length * precondition * drift_term
            + math.sqrt(2.0 * step_length) * jnp.sqrt(precondition) * noise[step_num]
        )
    return (current, moment)


def solution(mesh):
    return jax.shard_map(
        on_device,
        mesh=mesh,
        in_specs=(
            P("freq", "param", None),
            P("freq", "param", None),
            P(None, "freq", "param", None),
            P(None, "freq", "param", None),
            P("freq", None),
            P("freq", None),
            P("freq"),
        ),
        out_specs=(P("freq", "param", None), P("freq", "param", None)),
        check_vma=False,
    )
```

```python
import functools
import math

import jax
import jax.numpy as jnp
from jax import lax
from jax.experimental import pallas as pl
from jax.experimental.pallas import tpu as pltpu
from jax.sharding import PartitionSpec as P

decay_rate = 0.9
step_length = 0.5
MESH = pl.DeviceIdType.MESH
LANES = 128
CHUNK_FREQS = 2
STAGE_TICKS = (0, 1, 3, 5, 7, 9, 10)


def spectral_table(time_len, freq_total):
    time_index = jnp.arange(time_len, dtype=jnp.int32)[:, None]
    wave_number = jnp.arange(freq_total, dtype=jnp.int32)[None, :] + 1
    phase_angle = (time_index * wave_number % time_len).astype(jnp.float32) * (
        2.0 * math.pi / time_len
    )
    columns_table = jnp.stack([jnp.cos(phase_angle), -jnp.sin(phase_angle)], axis=-1).reshape(
        time_len, 2 * freq_total
    )
    return (columns_table / math.sqrt(time_len)).astype(jnp.bfloat16)


def exchange_kernel(
    freq_count, chunk_freqs, stage_ticks,
    spec_ref, green_hbm, obs_ref, inv_ref, own_ref,
    obs_blocks, inv_blocks, green, field, acc, outgoing, incoming, wtd, adj,
    green_sem, spec_send, spec_recv, line_send, line_recv, adj_send, adj_recv, local_sem,
):
    freq_me = lax.axis_index("freq")
    param_me = lax.axis_index("param")
    freq_loc, rows = spec_ref.shape[1], spec_ref.shape[2]
    half_rows = rows // 2
    sensors = green.shape[3]
    col_blocks = sensors // LANES
    chunk_blocks = chunk_freqs * col_blocks
    chunks = freq_loc // chunk_freqs
    core = lax.rem(param_me, 2)
    chip = param_me // 2
    side = chip // 2
    outer = (chip + side) % 2 == 0
    inner = (chip + side) % 2 == 1
    core_peer = param_me + 1 - 2 * core
    chip_peer = param_me + 2 * (1 - 2 * lax.rem(chip, 2))
    mid_peer = param_me + 2 * (1 - 2 * side)
    core_len, mid_len = chunk_blocks // 2, chunk_blocks // 4
    core_off = core * core_len
    mid_off = core_off + side * mid_len

    def freq_peer(d):
        return lax.rem(freq_me + d, freq_count)

    def freq_source(d):
        return lax.rem(freq_me + freq_count - d, freq_count)

    barrier = pltpu.get_barrier_semaphore()
    for d in range(1, freq_count):
        pl.semaphore_signal(barrier, inc=1, device_id={"freq": freq_peer(d)}, device_id_type=MESH)
    for peer in (core_peer, chip_peer):
        pl.semaphore_signal(barrier, inc=1, device_id={"param": peer}, device_id_type=MESH)

    @pl.when(inner)
    def _():
        pl.semaphore_signal(barrier, inc=1, device_id={"param": mid_peer}, device_id_type=MESH)

    def green_copy(i):
        part = pl.ds(i * chunk_freqs, chunk_freqs)
        return pltpu.make_async_copy(green_hbm.at[:, part], green.at[:, part], green_sem.at[i])

    def own_spec_copy():
        return pltpu.make_async_copy(spec_ref.at[freq_me], field.at[:, freq_me], local_sem.at[0])

    def spec_copy(i, d):
        part = pl.ds(i * chunk_freqs, chunk_freqs)
        return pltpu.make_async_remote_copy(
            src_ref=spec_ref.at[freq_peer(d), part],
            dst_ref=field.at[part, freq_me],
            send_sem=spec_send.at[d - 1, i],
            recv_sem=spec_recv.at[d - 1, i],
            device_id={"freq": freq_peer(d)},
            device_id_type=MESH,
        )

    def param_copy(k, i, src, dst, peer):
        return pltpu.make_async_remote_copy(
            src_ref=src,
            dst_ref=dst,
            send_sem=line_send.at[k, i],
            recv_sem=line_recv.at[k, i],
            device_id={"param": peer},
            device_id_type=MESH,
        )

    def core_reduce(i):
        src = outgoing[0].at[pl.ds(i * chunk_blocks + (1 - core) * core_len, core_len)]
        return param_copy(0, i, src, incoming[0].at[pl.ds(i * core_len, core_len)], core_peer)

    def chip_reduce(i):
        part = pl.ds(i * core_len, core_len)
        return param_copy(1, i, outgoing[1].at[part], incoming[1].at[part], chip_peer)

    def mid_reduce(i):
        part = pl.ds(i * mid_len, mid_len)
        return param_copy(2, i, outgoing[2].at[part], incoming[2].at[part], mid_peer)

    def mid_gather(i):
        part = wtd.at[pl.ds(i * chunk_blocks + mid_off, mid_len)]
        return param_copy(3, i, part, part, mid_peer)

    def chip_gather(i):
        part = wtd.at[pl.ds(i * chunk_blocks + core_off, core_len)]
        return param_copy(4, i, part, part, chip_peer)

    def core_gather(i):
        part = wtd.at[pl.ds(i * chunk_blocks + core_off, core_len)]
        return param_copy(5, i, part, part, core_peer)

    def adj_copy(i, d):
        part = pl.ds(i * chunk_freqs, chunk_freqs)
        return pltpu.make_async_remote_copy(
            src_ref=adj.at[part, freq_peer(d)],
            dst_ref=own_ref.at[freq_me, part],
            send_sem=adj_send.at[d - 1, i],
            recv_sem=adj_recv.at[d - 1, i],
            device_id={"freq": freq_peer(d)},
            device_id_type=MESH,
        )

    def own_adj_copy(i):
        part = pl.ds(i * chunk_freqs, chunk_freqs)
        return pltpu.make_async_copy(
            adj.at[part, freq_me], own_ref.at[freq_me, part], local_sem.at[i + 1]
        )

    own_spec_copy().start()

    @pl.loop(0, chunks)
    def _(i):
        green_copy(i).start()

    for f in range(freq_loc):
        for b in range(col_blocks):
            lanes = slice(b * LANES, (b + 1) * LANES)
            inv_blocks[f * col_blocks + b] = inv_ref[f : f + 1, lanes]
            for ri in range(2):
                lanes = slice(ri * sensors + b * LANES, ri * sensors + (b + 1) * LANES)
                obs_blocks[f * col_blocks + b, ri : ri + 1] = obs_ref[f : f + 1, lanes]

    pl.semaphore_wait(barrier, freq_count + 1 + (chip + side) % 2)

    @pl.loop(0, chunks)
    def _(i):
        for d in range(1, freq_count):
            spec_copy(i, d).start()

    own_spec_copy().wait()

    def combine(first, second, sign):
        pieces = []
        for j in range(freq_count):
            for ri in range(2):
                here = j * rows + ri * half_rows
                there = j * rows + (1 - ri) * half_rows
                a = first[here : here + half_rows]
                b = second[there : there + half_rows]
                pieces.append(a + b if (ri == 1) == (sign > 0) else a - b)
        return jnp.concatenate(pieces, axis=0)

    def forward(i):
        green_copy(i).wait()
        for d in range(1, freq_count):
            spec_copy(i, d).wait_recv()
        for g in range(chunk_freqs):
            f = i * chunk_freqs + g
            x = field[f].reshape(freq_count * rows, field.shape[3])
            first = jnp.dot(x, green[0, f], preferred_element_type=jnp.float32)
            second = jnp.dot(x, green[1, f], preferred_element_type=jnp.float32)
            data = combine(first, second, 1)
            for b in range(col_blocks):
                block = data[:, b * LANES : (b + 1) * LANES]
                acc[f * col_blocks + b] = block
                outgoing[0][f * col_blocks + b] = block.astype(jnp.bfloat16)
        core_reduce(i).start()

    def pass_inward(i):
        core_reduce(i).wait_recv()
        kept = pl.ds(i * chunk_blocks + core_off, core_len)
        part = pl.ds(i * core_len, core_len)
        total = acc[kept] + incoming[0][part].astype(jnp.float32)

        @pl.when(inner)
        def _():
            acc[kept] = total

        @pl.when(outer)
        def _():
            outgoing[1][part] = total.astype(jnp.bfloat16)
            chip_reduce(i).start()

    def cross(i):
        @pl.when(inner)
        def _():
            chip_reduce(i).wait_recv()
            kept = pl.ds(i * chunk_blocks + core_off, core_len)
            part = pl.ds(i * core_len, core_len)
            acc[kept] = acc[kept] + incoming[1][part].astype(jnp.float32)
            away = pl.ds(i * chunk_blocks + core_off + (1 - side) * mid_len, mid_len)
            outgoing[2][pl.ds(i * mid_len, mid_len)] = acc[away].astype(jnp.bfloat16)
            mid_reduce(i).start()

    def weigh(i):
        @pl.when(inner)
        def _():
            mid_reduce(i).wait_recv()
            for n in range(mid_len):
                b = i * chunk_blocks + mid_off + n
                total = acc[b] + incoming[2][i * mid_len + n].astype(jnp.float32)
                target = obs_blocks[b]
                weight = inv_blocks[b]
                pieces = []
                for j in range(freq_count):
                    for ri in range(2):
                        here = j * rows + ri * half_rows
                        pieces.append(
                            weight * (total[here : here + half_rows] - target[ri : ri + 1])
                        )
                wtd[b] = jnp.concatenate(pieces, axis=0).astype(jnp.bfloat16)
            mid_gather(i).start()

    def pass_outward(i):
        @pl.when(inner)
        def _():
            mid_gather(i).wait_recv()
            chip_gather(i).start()
            core_gather(i).start()

    def share(i):
        @pl.when(outer)
        def _():
            chip_gather(i).wait_recv()
            core_gather(i).start()

    def backward(i):
        core_gather(i).wait_recv()
        dims = (((1,), (1,)), ((), ()))
        for g in range(chunk_freqs):
            f = i * chunk_freqs + g
            w = jnp.concatenate([wtd[f * col_blocks + b] for b in range(col_blocks)], axis=1)
            first = lax.dot_general(w, green[0, f], dims, preferred_element_type=jnp.float32)
            second = lax.dot_general(w, green[1, f], dims, preferred_element_type=jnp.float32)
            back = combine(first, second, -1).astype(jnp.bfloat16)
            adj[f] = back.reshape(freq_count, rows, back.shape[1])
        for d in range(1, freq_count):
            adj_copy(i, d).start()
        own_adj_copy(i).start()

    stages = (forward, pass_inward, cross, weigh, pass_outward, share, backward)

    @pl.loop(0, chunks + stage_ticks[-1])
    def _(tick):
        for lag, stage in zip(stage_ticks, stages):
            @pl.when((tick >= lag) & (tick < chunks + lag))
            def _():
                stage(tick - lag)

    @pl.loop(0, chunks)
    def _(i):
        for d in range(1, freq_count):
            spec_copy(i, d).wait_send()
        core_reduce(i).wait_send()
        core_gather(i).wait_send()

        @pl.when(outer)
        def _():
            chip_reduce(i).wait_send()

        @pl.when(inner)
        def _():
            mid_reduce(i).wait_send()
            mid_gather(i).wait_send()
            chip_gather(i).wait_send()

        for d in range(1, freq_count):
            adj_copy(i, d).wait_send()
            adj_copy(i, d).wait_recv()
        own_adj_copy(i).wait()


def exchange(spec, green, observed, inv_noise, call_id):
    freq_count, freq_loc, rows, slab = spec.shape
    sensors = green.shape[3]
    col_blocks = sensors // LANES
    chunk_blocks = CHUNK_FREQS * col_blocks
    chunks = freq_loc // CHUNK_FREQS
    blocks = freq_loc * col_blocks
    all_rows = freq_count * rows
    bf16, f32 = jnp.bfloat16, jnp.float32
    dma = pltpu.SemaphoreType.DMA
    vmem = pl.BlockSpec(memory_space=pltpu.VMEM)
    flops = 16 * freq_loc * all_rows * slab * sensors
    return pl.pallas_call(
        functools.partial(exchange_kernel, freq_count, CHUNK_FREQS, STAGE_TICKS),
        out_shape=jax.ShapeDtypeStruct(spec.shape, bf16),
        in_specs=[vmem, pl.BlockSpec(memory_space=pltpu.HBM), vmem, vmem],
        out_specs=vmem,
        scratch_shapes=[
            pltpu.VMEM((blocks, 2, LANES), f32),
            pltpu.VMEM((blocks, 1, LANES), f32),
            pltpu.VMEM(green.shape, bf16),
            pltpu.VMEM((freq_loc, freq_count, rows, slab), bf16),
            pltpu.VMEM((blocks, all_rows, LANES), f32),
            [pltpu.VMEM((blocks // part, all_rows, LANES), bf16) for part in (1, 2, 4)],
            [pltpu.VMEM((blocks // part, all_rows, LANES), bf16) for part in (2, 2, 4)],
            pltpu.VMEM((blocks, all_rows, LANES), bf16),
            pltpu.VMEM((freq_loc, freq_count, rows, slab), bf16),
            dma((chunks,)),
            dma((freq_count - 1, chunks)),
            dma((freq_count - 1, chunks)),
            dma((6, chunks)),
            dma((6, chunks)),
            dma((freq_count - 1, chunks)),
            dma((freq_count - 1, chunks)),
            dma((chunks + 1,)),
        ],
        compiler_params=pltpu.CompilerParams(
            collective_id=call_id, has_side_effects=True, vmem_limit_bytes=20 * 2**20
        ),
        cost_estimate=pl.CostEstimate(
            flops=flops, bytes_accessed=2 * green.size, transcendentals=0
        ),
    )(spec, green, observed, inv_noise)


def fits_kernel(chain_shape, green_shape):
    chains_loc, slab = chain_shape[0], chain_shape[1]
    param_count = lax.axis_size("param")
    blocks = CHUNK_FREQS * (green_shape[3] // LANES)
    return (
        2 * chains_loc % 16 == 0
        and slab % LANES == 0
        and green_shape[3] % LANES == 0
        and green_shape[1] % CHUNK_FREQS == 0
        and param_count == 8
        and lax.axis_size("freq") > 1
        and blocks % 4 == 0
    )


def kernel_steps(chain_state, second_moment, noise, green, observed, inv_noise, temper):
    chains_loc, slab_rows, time_len = chain_state.shape
    freq_loc = green.shape[1]
    freq_count = lax.axis_size("freq")
    freq_total = freq_loc * freq_count
    table = spectral_table(time_len, freq_total)
    temper_cols = temper[:, None, None]
    current = chain_state
    moment = second_moment
    for step_num in range(noise.shape[0]):
        spec = jnp.einsum(
            "cpt,tj->jcp",
            current.astype(jnp.bfloat16),
            table,
            preferred_element_type=jnp.float32,
        ).astype(jnp.bfloat16)
        spec = spec.reshape(freq_count, freq_loc, 2 * chains_loc, slab_rows)
        own_adjoint = exchange(spec, green, observed, inv_noise, step_num)
        gradient = jnp.einsum(
            "jcp,tj->cpt",
            own_adjoint.reshape(2 * freq_total, chains_loc, slab_rows),
            table,
            preferred_element_type=jnp.float32,
        )
        drift_term = temper_cols * gradient + current
        moment = decay_rate * moment + (1.0 - decay_rate) * drift_term * drift_term
        precondition = lax.rsqrt(moment)
        current = (
            current
            - step_length * precondition * drift_term
            + math.sqrt(2.0 * step_length) * jnp.sqrt(precondition) * noise[step_num]
        )
    return (current, moment)


def on_device(chain_state, second_moment, noise, green, observed, inv_noise, temper):
    if fits_kernel(chain_state.shape, green.shape):
        return kernel_steps(
            chain_state, second_moment, noise, green, observed, inv_noise, temper
        )
    chains_loc, slab_rows, time_len = chain_state.shape
    freq_loc = green.shape[1]
    freq_count = lax.axis_size("freq")
    freq_total = freq_loc * freq_count
    chains = chains_loc * freq_count
    forward_table = spectral_table(time_len, freq_total)
    inverse_table = forward_table.T
    green_re = green[0]
    green_im = green[1]
    upper_rows = jnp.concatenate([green_re, green_im], axis=2)
    lower_rows = jnp.concatenate([-green_im, green_re], axis=2)
    kernel = jnp.concatenate([upper_rows, lower_rows], axis=1)
    weights = jnp.concatenate([inv_noise, inv_noise], axis=1)
    temper_cols = temper[:, None, None]
    current = chain_state
    moment = second_moment
    for step_num in range(noise.shape[0]):
        low_state = current.astype(jnp.bfloat16)
        local_spec = jnp.dot(
            low_state.reshape(chains_loc * slab_rows, time_len),
            forward_table,
            preferred_element_type=jnp.float32,
        )
        local_spec = local_spec.astype(jnp.bfloat16).reshape(chains_loc, slab_rows, 2 * freq_total)
        spectrum = lax.all_to_all(local_spec, "freq", split_axis=2, concat_axis=0, tiled=True)
        mixed_spec = (
            spectrum.reshape(chains, slab_rows, freq_loc, 2)
            .transpose(2, 0, 3, 1)
            .reshape(freq_loc, chains, 2 * slab_rows)
        )
        partial_data = jnp.einsum(
            "fcq,fqs->fcs", mixed_spec, kernel, preferred_element_type=jnp.float32
        )
        predicted = lax.psum(partial_data.astype(jnp.bfloat16), "param").astype(jnp.float32)
        weighted = (weights[:, None, :] * (predicted - observed[:, None, :])).astype(jnp.bfloat16)
        adjoint = jnp.einsum(
            "fcs,fqs->fcq", weighted, kernel, preferred_element_type=jnp.float32
        ).astype(jnp.bfloat16)
        adjoint = (
            adjoint.reshape(freq_loc, chains, 2, slab_rows)
            .transpose(1, 3, 0, 2)
            .reshape(chains, slab_rows, 2 * freq_loc)
        )
        own_adjoint = lax.all_to_all(adjoint, "freq", split_axis=0, concat_axis=2, tiled=True)
        gradient = jnp.dot(
            own_adjoint.reshape(chains_loc * slab_rows, 2 * freq_total),
            inverse_table,
            preferred_element_type=jnp.float32,
        )
        gradient = gradient.reshape(chains_loc, slab_rows, time_len)
        drift_term = temper_cols * gradient + current
        moment = decay_rate * moment + (1.0 - decay_rate) * drift_term * drift_term
        precondition = lax.rsqrt(moment)
        current = (
            current
            - step_length * precondition * drift_term
            + math.sqrt(2.0 * step_length) * jnp.sqrt(precondition) * noise[step_num]
        )
    return (current, moment)


def solution(mesh):
    return jax.shard_map(
        on_device,
        mesh=mesh,
        in_specs=(
            P("freq", "param", None),
            P("freq", "param", None),
            P(None, "freq", "param", None),
            P(None, "freq", "param", None),
            P("freq", None),
            P("freq", None),
            P("freq"),
        ),
        out_specs=(P("freq", "param", None), P("freq", "param", None)),
        check_vma=False,
    )
```
